128 devices in a mesh: section: 16 (over z_lo, y, core), dp: 4 (over x), tensor: 2 (over z_hi).
Axes of the slice: x: 4, y: 4, z: 4 (z_hi: 2, z_lo: 2; z = z_hi * 2 + z_lo), core: 2. Of those that a mesh axis runs over, the one named last changes fastest.
Arguments:
- inputs: bfloat16 [16, 4, 512, 2048], P('section', None, ('dp', 'tensor')), may hold values from -6 to 6
- cotangents: bfloat16 [16, 2, 512, 2048], P('section', None, ('dp', 'tensor')), may hold values from -6 to 6
- lengths: int32 [16, 4, 4], P('section'), may hold values from 1 to 128, as said below
- query_weight: bfloat16 [16, 2, 2048, 2048], P('section', None, None, ('dp', 'tensor')), as said below
- key_weight: bfloat16 [16, 2, 2048, 2048], P('section', None, None, ('dp', 'tensor')), as said below
- value_weight: bfloat16 [16, 2, 2048, 2048], P('section', None, None, ('dp', 'tensor')), as said below
- out_weight: bfloat16 [16, 2, 2048, 2048], P('section', None, ('dp', 'tensor')), as said below
- norm_gain: float32 [16, 2, 2048], P('section'), as said below
Outputs:
- sent: bfloat16 [16, 4, 512, 2048], P('section', None, ('dp', 'tensor'))
- grad_query: bfloat16 [16, 2048, 2048], P('section', None, ('dp', 'tensor'))
- grad_key: bfloat16 [16, 2048, 2048], P('section', None, ('dp', 'tensor'))
- grad_value: bfloat16 [16, 2048, 2048], P('section', None, ('dp', 'tensor'))
- grad_out: bfloat16 [16, 2048, 2048], P('section', ('dp', 'tensor'))
- grad_gain: bfloat16 [16, 2048], P('section')
The draws below stay inside these ranges and needn't reach their ends.
Inputs may be any that keep to these rules, and one draw needn't show every extreme that they name: `lengths`: each caption's length; 128 is reached in every draw. `query_weight`: entry [s, 1] equals entry [15 - s, 0] for every s. `key_weight`: entry [s, 1] equals entry [15 - s, 0] for every s. `value_weight`: entry [s, 1] equals entry [15 - s, 0] for every s. `out_weight`: entry [s, 1] equals entry [15 - s, 0] for every s. `norm_gain`: entry [s, 1] equals entry [15 - s, 0] for every s; positive.
All inputs are finite; a program needn't handle non-finite values.
Results may differ from the reference program's by a relative error of at most 0.011.
Values may be sent and summed in bfloat16 or wider, within the bound.
No kernel may reach another device: no remote copies, remote signals or barrier semaphores. Data moves between devices by JAX's collectives and lax.ppermute only.
A program may use at most 128 MiB of HBM per device.

```python
import jax
import jax.numpy as jnp
from jax import lax

D = 2048
HD = 64
L = 128
SECTIONS = 16
CAPTIONS = 4
TOKENS = 512
HT = 2048
N_DP = 4
N_TENSOR = 2


def mirrored(key, first_dim, second_dim, fan_in):
    base = jax.random.normal(key, (SECTIONS, first_dim, second_dim), jnp.float32) * fan_in ** (-0.5)
    return jnp.stack([base, jnp.flip(base, axis=0)], axis=1).astype(jnp.bfloat16)


def draw_query_weight(key, part):
    return mirrored(jax.random.fold_in(key, 11), D, HT, D)


def draw_key_weight(key, part):
    return mirrored(jax.random.fold_in(key, 12), D, HT, D)


def draw_value_weight(key, part):
    return mirrored(jax.random.fold_in(key, 13), D, HT, D)


def draw_out_weight(key, part):
    return mirrored(jax.random.fold_in(key, 14), HT, D, HT)


def draw_norm_gain(key, part):
    base = jax.random.uniform(jax.random.fold_in(key, 15), (SECTIONS, D), jnp.float32, 0.5, 1.5)
    return jnp.stack([base, jnp.flip(base, axis=0)], axis=1).astype(jnp.float32)


def draw_lengths(key, part):
    total = SECTIONS * 4 * CAPTIONS
    drawn = jax.random.randint(jax.random.fold_in(key, 16), (total,), 1, L + 1)
    where_max = jax.random.randint(jax.random.fold_in(key, 17), (), 0, total)
    drawn = drawn.at[where_max].set(L)
    return drawn.reshape(SECTIONS, 4, CAPTIONS).astype(jnp.int32)


def level_of(rng, extent, cuts, smallest, top_value):
    def one(position, shards_of):
        draws = jax.random.uniform(jax.random.fold_in(jax.random.fold_in(rng, 6), position), (shards_of,), jnp.float32, smallest / len(cuts), top_value / len(cuts))
        return jnp.repeat(jnp.exp(draws), extent[position] // shards_of).reshape((-1,) + (1,) * (len(extent) - position - 1))

    factor_of = one(*cuts[0])
    for cut in cuts[1:]:
        factor_of = factor_of * one(*cut)
    return factor_of


def normal_values(key, extent, scale, limit, shards=(), kind=jnp.bfloat16):
    result = jax.random.normal(key, extent, jnp.float32) * scale
    if len(shards) > 0:
        result = level_of(key, extent, shards, -0.22, 0.18) * result
    return jnp.clip(result, min=-limit, max=limit).astype(kind)


def setup_inputs(seed: int = 0) -> dict:
    streams_of = jax.random.split(jax.random.key(seed), 9)
    inputs = normal_values(streams_of[0], (SECTIONS, 4, TOKENS, D), 1.0, 6.0, ((0, 16), (2, 8)))
    cotangents = normal_values(streams_of[1], (SECTIONS, 2, TOKENS, D), 1.0, 6.0, ((0, 16), (2, 8)))
    lengths = draw_lengths(jax.random.fold_in(streams_of[8], 71), 0)
    query_weight = draw_query_weight(jax.random.fold_in(streams_of[8], 71), 0)
    key_weight = draw_key_weight(jax.random.fold_in(streams_of[8], 71), 0)
    value_weight = draw_value_weight(jax.random.fold_in(streams_of[8], 71), 0)
    out_weight = draw_out_weight(jax.random.fold_in(streams_of[8], 71), 0)
    norm_gain = draw_norm_gain(jax.random.fold_in(streams_of[8], 71), 0)
    return {"inputs": inputs, "cotangents": cotangents, "lengths": lengths, "query_weight": query_weight, "key_weight": key_weight, "value_weight": value_weight, "out_weight": out_weight, "norm_gain": norm_gain}


EPS = 1e-06
NEG_FILL = -1e+30

def normalize(tok_rows, gain_vec):
    widened = tok_rows.astype(jnp.float32)
    inverse = lax.rsqrt(lax.optimization_barrier(jnp.mean(widened * widened, axis=1, keepdims=True)) + EPS)
    normed = (widened * inverse * gain_vec).astype(jnp.bfloat16)
    return (widened, inverse, normed)

def split_heads(tensor, length, head_dim):
    return tensor.astype(jnp.float32).reshape(tensor.shape[0] // length, length, tensor.shape[1] // head_dim, head_dim)

def merge_heads(tensor):
    return tensor.reshape(tensor.shape[0] * tensor.shape[1], tensor.shape[2] * tensor.shape[3])

def project(left, right):
    return jnp.dot(left, right, preferred_element_type=jnp.float32)

def outer_sum(left, right):
    return jnp.dot(left.T, right, preferred_element_type=jnp.float32).astype(jnp.bfloat16)

def attend(normed, weight_set, caption_lens, length, head_dim):
    gain_vec, query_part, key_part, value_part, out_part = weight_set
    queries = project(normed, query_part).astype(jnp.bfloat16)
    key_rows = project(normed, key_part).astype(jnp.bfloat16)
    value_rows = project(normed, value_part).astype(jnp.bfloat16)
    factor = head_dim ** (-0.5)
    scores = jnp.einsum('cqhd,ckhd->chqk', split_heads(queries, length, head_dim), split_heads(key_rows, length, head_dim)) * factor
    visible = (jnp.arange(length, dtype=jnp.int32)[None, :] < caption_lens[:, None])[:, None, None, :]
    scores = jnp.where(visible, scores, NEG_FILL)
    chances = jax.nn.softmax(scores, axis=-1)
    weights = chances.astype(jnp.bfloat16)
    mixture = merge_heads(jnp.einsum('chqk,ckhd->cqhd', weights.astype(jnp.float32), split_heads(value_rows, length, head_dim))).astype(jnp.bfloat16)
    return (queries, key_rows, value_rows, chances, weights, mixture)

def attend_back(pieces, upstream, weight_set, length, head_dim):
    queries, key_rows, value_rows, chances, weights, mixture = pieces
    gain_vec, query_part, key_part, value_part, out_part = weight_set
    factor = head_dim ** (-0.5)
    grad_mix = jnp.dot(upstream, out_part.T, preferred_element_type=jnp.float32).astype(jnp.bfloat16)
    grad_split = split_heads(grad_mix, length, head_dim)
    grad_chances = jnp.einsum('cqhd,ckhd->chqk', grad_split, split_heads(value_rows, length, head_dim))
    grad_value = merge_heads(jnp.einsum('chqk,cqhd->ckhd', weights.astype(jnp.float32), grad_split)).astype(jnp.bfloat16)
    grad_scores = (chances * (grad_chances - lax.optimization_barrier(jnp.sum(grad_chances * chances, axis=-1, keepdims=True))) * factor).astype(jnp.bfloat16)
    grad_query = merge_heads(jnp.einsum('chqk,ckhd->cqhd', grad_scores.astype(jnp.float32), split_heads(key_rows, length, head_dim))).astype(jnp.bfloat16)
    grad_key = merge_heads(jnp.einsum('chqk,cqhd->ckhd', grad_scores.astype(jnp.float32), split_heads(queries, length, head_dim))).astype(jnp.bfloat16)
    grad_normed = jnp.dot(grad_query, query_part.T, preferred_element_type=jnp.float32)
    grad_normed = grad_normed + jnp.dot(grad_key, key_part.T, preferred_element_type=jnp.float32)
    grad_normed = grad_normed + jnp.dot(grad_value, value_part.T, preferred_element_type=jnp.float32)
    return (grad_normed, grad_query, grad_key, grad_value)

def norm_back(widened, inverse, gain_vec, grad_normed):
    scaled = grad_normed * gain_vec
    gain_part = lax.optimization_barrier(jnp.sum(grad_normed * widened * inverse, axis=0))
    grad_rows = inverse * scaled - widened * inverse * inverse * inverse * lax.optimization_barrier(jnp.mean(scaled * widened, axis=1, keepdims=True))
    return (grad_rows, gain_part)

def group_set(weight_set, group, width):
    gain_vec, query_part, key_part, value_part, out_part = weight_set
    low = group * width
    high = low + width
    return (gain_vec, query_part[:, low:high], key_part[:, low:high], value_part[:, low:high], out_part[low:high, :])

def forward_block(tok_rows, weight_set, caption_lens):
    groups = N_DP * N_TENSOR
    width = weight_set[1].shape[1] // groups
    widened, inverse, normed = normalize(tok_rows, weight_set[0])
    total = widened
    for group in range(groups):
        subset = group_set(weight_set, group, width)
        pieces = attend(normed, subset, caption_lens, L, HD)
        rounded = lax.optimization_barrier(project(pieces[5], subset[4]).astype(jnp.bfloat16))
        total = total + rounded.astype(jnp.float32)
    return total.astype(jnp.bfloat16)

def backward_block(tok_rows, upstream, weight_set, caption_lens):
    groups = N_DP * N_TENSOR
    width = weight_set[1].shape[1] // groups
    widened, inverse, normed = normalize(tok_rows, weight_set[0])
    total = upstream.astype(jnp.float32)
    gain_total = jnp.zeros(weight_set[0].shape, jnp.float32)
    query_grads, key_grads, value_grads, out_grads = ([], [], [], [])
    for group in range(groups):
        subset = group_set(weight_set, group, width)
        pieces = attend(normed, subset, caption_lens, L, HD)
        grad_normed, grad_query, grad_key, grad_value = attend_back(pieces, upstream, subset, L, HD)
        grad_rows, gain_part = norm_back(widened, inverse, subset[0], grad_normed)
        rounded = lax.optimization_barrier(grad_rows.astype(jnp.bfloat16))
        total = total + rounded.astype(jnp.float32)
        gain_total = gain_total + gain_part
        query_grads.append(outer_sum(normed, grad_query))
        key_grads.append(outer_sum(normed, grad_key))
        value_grads.append(outer_sum(normed, grad_value))
        out_grads.append(outer_sum(pieces[5], upstream))
    grads = (jnp.concatenate(query_grads, axis=1), jnp.concatenate(key_grads, axis=1), jnp.concatenate(value_grads, axis=1), jnp.concatenate(out_grads, axis=0), gain_total.astype(jnp.bfloat16))
    return (total.astype(jnp.bfloat16), grads)

def reference(inputs, cotangents, lengths, query_weight, key_weight, value_weight, out_weight, norm_gain):
    sections = inputs.shape[0]
    sent = [[None, None, None, None] for section in range(sections)]
    down_grads = []
    up_grads = []
    for section in range(sections):
        down_set = (norm_gain[section, 0], query_weight[section, 0], key_weight[section, 0], value_weight[section, 0], out_weight[section, 0])
        up_set = (norm_gain[section, 1], query_weight[section, 1], key_weight[section, 1], value_weight[section, 1], out_weight[section, 1])
        sent[(section + 1) % sections][0] = forward_block(inputs[section, 0], down_set, lengths[section, 0])
        sent[(section - 1) % sections][1] = forward_block(inputs[section, 1], up_set, lengths[section, 1])
        grad_input, grads = backward_block(inputs[section, 2], cotangents[section, 0], down_set, lengths[section, 2])
        sent[(section - 1) % sections][2] = grad_input
        down_grads.append(grads)
        grad_input, grads = backward_block(inputs[section, 3], cotangents[section, 1], up_set, lengths[section, 3])
        sent[(section + 1) % sections][3] = grad_input
        up_grads.append(grads)
    sent_all = jnp.stack([jnp.stack(sent[section]) for section in range(sections)])
    merged = []
    for which in range(5):
        rows_out = []
        for section in range(sections):
            mine = down_grads[section][which].astype(jnp.float32)
            theirs = up_grads[sections - 1 - section][which].astype(jnp.float32)
            rows_out.append((mine + theirs).astype(jnp.bfloat16))
        merged.append(jnp.stack(rows_out))
    return (sent_all, merged[0], merged[1], merged[2], merged[3], merged[4])
```

```python
import jax
import jax.numpy as jnp
from jax import lax
from jax.experimental import pallas as pl
from jax.experimental.pallas import tpu as pltpu
from jax.sharding import PartitionSpec as P

HD = 64
L = 128
D = 2048
W = 256
ROWS = 64
HEADS = W // HD
CAPS = 4
TOK = CAPS * L
EPS = 1e-06
NEG_FILL = -1e30
FACTOR = HD ** (-0.5)
BF = jnp.bfloat16
F32 = jnp.float32


def along_x(a, by):
    n = lax.axis_size("dp")
    return lax.ppermute(a, "dp", [(i, (i + by) % n) for i in range(n)])


def across_z(a):
    return lax.ppermute(a, "tensor", [(0, 1), (1, 0)])


def to_section(a, where):
    n = lax.axis_size("section")
    return lax.ppermute(a, "section", [(i, where(i) % n) for i in range(n)])


def to_section_and_x(a, section_by, x_by):
    ns, nx = lax.axis_size("section"), lax.axis_size("dp")
    route = []
    for s in range(ns):
        for x in range(nx):
            route.append((s * nx + x, ((s + section_by) % ns) * nx + (x + x_by) % nx))
    return lax.ppermute(a, ("section", "dp"), route)


def gather_z_first(m):
    z = across_z(m)
    got = {(0, 0): m, (0, 1): z}
    for i in (1, 3, 2):
        got[i, 0] = along_x(m, -i)
    for i in (1, 3, 2):
        got[i, 1] = along_x(z, -i)
    return got


def gather_x_first(m):
    got = {(0, 0): m}
    for i in (1, 3, 2):
        got[i, 0] = along_x(m, -i)
    for i in (0, 1, 3, 2):
        got[i, 1] = across_z(got[i, 0])
    return got


def in_pieces(got):
    return [got[i, j] for i in range(CAPS) for j in range(2)]


def dot(a, b, ca, cb):
    return lax.dot_general(a, b, (((ca,), (cb,)), ((), ())), preferred_element_type=F32)


def visible_lanes(lens_ref, c):
    x = lax.axis_index("dp")
    t = lax.axis_index("tensor")
    length = lens_ref[lax.rem(x + c, CAPS)]
    col = lax.broadcasted_iota(jnp.int32, (1, L), 1)
    half = (col >= ROWS).astype(jnp.int32)
    position = col - half * ROWS + ROWS * (half + t - 2 * half * t)
    return position < length


def by_head(a):
    lane = lax.broadcasted_iota(jnp.int32, (1, W), 1)
    zero = jnp.zeros_like(a)
    return jnp.concatenate(
        [jnp.where((lane >= h * HD) & (lane < (h + 1) * HD), a, zero) for h in range(HEADS)], axis=0
    )


def heads_back(a):
    lane = lax.broadcasted_iota(jnp.int32, (1, W), 1)
    out = a[:L]
    for h in range(1, HEADS):
        out = jnp.where(lane >= h * HD, a[h * L : (h + 1) * L], out)
    return out


def normed_rows(piece_refs, gain_ref, normed_ref, lead):
    for p, ref in enumerate(piece_refs):

        def step(n, carry, ref=ref, p=p):
            at = pl.multiple_of(n * 16, 16)
            rows = ref[(*lead, pl.ds(at, 16), slice(None))].astype(F32)
            inverse = lax.rsqrt(jnp.mean(rows * rows, axis=1, keepdims=True) + EPS)
            normed_ref[pl.ds(p * ROWS + at, 16), :] = (rows * inverse * gain_ref[...]).astype(BF)
            return carry

        lax.fori_loop(0, ROWS // 16, step, 0)


def softmaxed(q, k, seen):
    scores = dot(by_head(q), k, 1, 1) * FACTOR
    scores = jnp.where(seen, scores, NEG_FILL)
    raised = jnp.exp(scores - jnp.max(scores, axis=1, keepdims=True))
    return raised / jnp.sum(raised, axis=1, keepdims=True)


def split_store(block, tile, keep_ref, send_ref):
    for i in range(CAPS):
        keep_ref[i, :, tile] = block[i * L : i * L + ROWS].astype(BF)
        send_ref[i, :, tile] = block[i * L + ROWS : (i + 1) * L].astype(BF)


def forward_kernel(lens_ref, *refs):
    pieces = refs[:8]
    gain_ref, wq, wk, wv, wo, keep_ref, send_ref, normed, q_s, k_s, v_s, mix_s = refs[8:]
    normed_rows(pieces, gain_ref, normed, ())
    q_s[...] = dot(normed[...], wq[...], 1, 0).astype(BF)
    k_s[...] = dot(normed[...], wk[...], 1, 0).astype(BF)
    v_s[...] = dot(normed[...], wv[...], 1, 0).astype(BF)

    def caption(c, carry):
        rows = pl.ds(pl.multiple_of(c * L, L), L)
        chances = softmaxed(q_s[rows, :], k_s[rows, :], visible_lanes(lens_ref, c))
        mix_s[rows, :] = heads_back(dot(chances.astype(BF), v_s[rows, :], 1, 0)).astype(BF)
        return carry

    lax.fori_loop(0, CAPS, caption, 0)

    def out_tile(n, carry):
        tile = pl.ds(pl.multiple_of(n * W, W), W)
        split_store(dot(mix_s[...], wo[:, tile], 1, 0), tile, keep_ref, send_ref)
        return carry

    lax.fori_loop(0, D // W, out_tile, 0)


def backward_kernel(lens_ref, *refs):
    pieces = refs[:8]
    gain_ref, wq, wk, wv, wo, keep_ref, send_ref, normed, up, dqkv, mix_s, q_s, k_s, v_s, dm_s = refs[8:]
    normed_rows(pieces, gain_ref, normed, (0,))
    for p, ref in enumerate(pieces):
        up[p * ROWS : (p + 1) * ROWS, :] = ref[1]
    q_s[...] = dot(normed[...], wq[...], 1, 0).astype(BF)
    k_s[...] = dot(normed[...], wk[...], 1, 0).astype(BF)
    v_s[...] = dot(normed[...], wv[...], 1, 0).astype(BF)
    dm_s[...] = dot(up[...], wo[...], 1, 1).astype(BF)

    def caption(c, carry):
        rows = pl.ds(pl.multiple_of(c * L, L), L)
        q, k, v = q_s[rows, :], k_s[rows, :], v_s[rows, :]
        chances = softmaxed(q, k, visible_lanes(lens_ref, c))
        weights = chances.astype(BF)
        mix_s[rows, :] = heads_back(dot(weights, v, 1, 0)).astype(BF)
        dm = by_head(dm_s[rows, :])
        grad_chances = dot(dm, v, 1, 1)
        dqkv[rows, 2 * W :] = dot(weights, dm, 0, 0).astype(BF)
        total = jnp.sum(grad_chances * chances, axis=1, keepdims=True)
        grad_scores = (chances * (grad_chances - total) * FACTOR).astype(BF)
        dqkv[rows, :W] = heads_back(dot(grad_scores, k, 1, 0)).astype(BF)
        dqkv[rows, W : 2 * W] = dot(grad_scores, by_head(q), 0, 0).astype(BF)
        return carry

    lax.fori_loop(0, CAPS, caption, 0)

    def out_tile(n, carry):
        tile = pl.ds(pl.multiple_of(n * W, W), W)
        block = dot(dqkv[:, :W], wq[tile, :], 1, 1)
        block = block + dot(dqkv[:, W : 2 * W], wk[tile, :], 1, 1)
        block = block + dot(dqkv[:, 2 * W :], wv[tile, :], 1, 1)
        split_store(block, tile, keep_ref, send_ref)
        return carry

    lax.fori_loop(0, D // W, out_tile, 0)


def once(shape, index):
    return pl.BlockSpec(shape, lambda i: index, pipeline_mode=pl.Buffered(1))


def whole(shape):
    return once(shape, (0,) * len(shape))


def weight_specs(slot):
    return [
        once((None, None, 1, D), (0, slot, 0, 0)),
        once((None, None, D, W), (0, slot, 0, 0)),
        once((None, None, D, W), (0, slot, 0, 0)),
        once((None, None, D, W), (0, slot, 0, 0)),
        once((None, None, W, D), (0, slot, 0, 0)),
    ]


def shape_of(*shape):
    return jax.ShapeDtypeStruct(shape, BF)


PARAMS = pltpu.CompilerParams(vmem_limit_bytes=40 * 1024 * 1024)


def forward_call(pieces, which, lens, weights, slot):
    return pl.pallas_call(
        forward_kernel,
        name="forward_block",
        grid=(1,),
        in_specs=[pl.BlockSpec(memory_space=pltpu.SMEM)]
        + [once((None, ROWS, D), (which, 0, 0))] * 8
        + weight_specs(slot),
        out_specs=[whole((CAPS, ROWS, D))] * 2,
        out_shape=[shape_of(CAPS, ROWS, D)] * 2,
        scratch_shapes=[pltpu.VMEM((TOK, D), BF)] + [pltpu.VMEM((TOK, W), BF)] * 4,
        compiler_params=PARAMS,
        cost_estimate=pl.CostEstimate(
            flops=2 * TOK * D * W * 4, bytes_accessed=8 * 1024 * 1024, transcendentals=TOK * L * 4
        ),
    )(lens, *pieces, *weights)


def backward_call(pieces, lens, weights, slot):
    return pl.pallas_call(
        backward_kernel,
        name="backward_block",
        grid=(1,),
        in_specs=[pl.BlockSpec(memory_space=pltpu.SMEM)]
        + [whole((2, ROWS, D))] * 8
        + weight_specs(slot),
        out_specs=[whole((CAPS, ROWS, D))] * 2
        + [whole((TOK, D))] * 2
        + [whole((TOK, 3 * W)), whole((TOK, W))],
        out_shape=[shape_of(CAPS, ROWS, D)] * 2
        + [shape_of(TOK, D)] * 2
        + [shape_of(TOK, 3 * W), shape_of(TOK, W)],
        scratch_shapes=[pltpu.VMEM((TOK, W), BF)] * 4,
        compiler_params=PARAMS,
        cost_estimate=pl.CostEstimate(
            flops=2 * TOK * D * W * 8, bytes_accessed=15 * 1024 * 1024, transcendentals=TOK * L * 4
        ),
    )(lens, *pieces, *weights)


def weight_grad_kernel(n1, u1, d1, m1, n2, u2, d2, m2, gq, gk, gv, go):
    block = dot(n1[...], d1[...], 0, 0) + dot(n2[...], d2[...], 0, 0)
    gq[...] = block[:, :W].astype(BF)
    gk[...] = block[:, W : 2 * W].astype(BF)
    gv[...] = block[:, 2 * W :].astype(BF)
    go[...] = (dot(m1[...], u1[...], 0, 0) + dot(m2[...], u2[...], 0, 0)).astype(BF)


def weight_grad_call(first, second):
    tile = pl.BlockSpec((TOK, W), lambda n: (0, n))
    fixed = [tile, tile, whole((TOK, 3 * W)), whole((TOK, W))]
    return pl.pallas_call(
        weight_grad_kernel,
        name="weight_grads",
        grid=(D // W,),
        in_specs=fixed * 2,
        out_specs=[pl.BlockSpec((None, W, W), lambda n: (0, n, 0))] * 3
        + [pl.BlockSpec((None, W, W), lambda n: (0, 0, n))],
        out_shape=[shape_of(1, D, W)] * 3 + [shape_of(1, W, D)],
        compiler_params=PARAMS,
        cost_estimate=pl.CostEstimate(
            flops=2 * 2 * TOK * D * W * 4, bytes_accessed=14 * 1024 * 1024, transcendentals=0
        ),
    )(*first, *second)


def half_summed(keep, send):
    came = across_z(send)
    return [keep[i].astype(F32) + came[i].astype(F32) for i in range(CAPS)]


def summed(keep, send):
    parts = half_summed(keep, send)
    total = parts[0]
    for i in (1, 3, 2):
        total = total + along_x(parts[i].astype(BF), i).astype(F32)
    return total


def summed_and_sent(keep, send, own, by):
    parts = half_summed(keep, send)
    total = to_section((parts[0] + own.astype(F32)).astype(BF), lambda s: s + by).astype(F32)
    for i in (1, 3, 2):
        total = total + to_section_and_x(parts[i].astype(BF), by, i).astype(F32)
    return total.astype(BF)


def input_grad(rows, upstream, gain, grad_normed):
    wide = rows.astype(F32)
    inverse = lax.rsqrt(jnp.mean(wide * wide, axis=1, keepdims=True) + EPS)
    scaled = grad_normed * gain
    gain_part = jnp.sum(grad_normed * wide * inverse, axis=0, keepdims=True)
    grad_rows = inverse * scaled - wide * inverse * inverse * inverse * jnp.mean(
        scaled * wide, axis=1, keepdims=True
    )
    return ((upstream.astype(F32) + grad_rows).astype(BF), gain_part)


def everyones(part):
    part = part + across_z(part)
    return part + along_x(part, 1) + along_x(part, -1) + along_x(part, 2)


def body(
    inputs, cotangents, lengths, query_weight, key_weight, value_weight, out_weight, norm_gain
):
    gains = norm_gain.reshape(1, 2, 1, D)
    weights = (gains, query_weight, key_weight, value_weight, out_weight)
    gain = norm_gain[0, 0][None]
    last = lax.axis_size("section") - 1

    mirror = lambda a: to_section(a, lambda s: last - s)
    far = mirror(jnp.stack([inputs[0, 3], cotangents[0, 1]]))
    far_lens = mirror(lengths[0, 3])
    near = jnp.stack([inputs[0, 2], cotangents[0, 0]])
    both = inputs[0, :2]

    near_got = in_pieces(gather_z_first(near))
    far_got = in_pieces(gather_z_first(far))
    both_got = in_pieces(gather_x_first(both))

    near_keep, near_send, *near_factors = backward_call(near_got, lengths[0, 2], weights, 0)
    far_keep, far_send, *far_factors = backward_call(far_got, far_lens, weights, 0)
    down_keep, down_send = forward_call(both_got, 0, lengths[0, 0], weights, 0)
    up_keep, up_send = forward_call(both_got, 1, lengths[0, 1], weights, 1)

    near_grad, near_gain = input_grad(near[0], near[1], gain, summed(near_keep, near_send))
    far_grad, far_gain = input_grad(far[0], far[1], gain, summed(far_keep, far_send))
    sent = jnp.stack(
        [
            summed_and_sent(down_keep, down_send, inputs[0, 0], 1),
            summed_and_sent(up_keep, up_send, inputs[0, 1], -1),
            to_section(near_grad, lambda s: s - 1),
            to_section(far_grad, lambda s: last + 1 - s),
        ]
    )[None]
    grad_gain = everyones(near_gain + far_gain).astype(BF)
    grads = weight_grad_call(near_factors, far_factors)
    return (sent, *grads, grad_gain)


def solution(mesh):
    return jax.shard_map(
        body,
        mesh=mesh,
        in_specs=(
            P("section", None, ("dp", "tensor"), None),
            P("section", None, ("dp", "tensor"), None),
            P("section", None, None),
            P("section", None, None, ("dp", "tensor")),
            P("section", None, None, ("dp", "tensor")),
            P("section", None, None, ("dp", "tensor")),
            P("section", None, ("dp", "tensor"), None),
            P("section", None, None),
        ),
        out_specs=(
            P("section", None, ("dp", "tensor"), None),
            P("section", None, ("dp", "tensor")),
            P("section", None, ("dp", "tensor")),
            P("section", None, ("dp", "tensor")),
            P("section", ("dp", "tensor"), None),
            P("section", None),
        ),
        check_vma=False,
    )
```

```python
import jax
import jax.numpy as jnp
from jax import lax
from jax.experimental import pallas as pl
from jax.experimental.pallas import tpu as pltpu
from jax.sharding import PartitionSpec as P

HD = 64
L = 128
D = 2048
W = 256
ROWS = 64
HEADS = W // HD
CAPS = 4
TOK = CAPS * L
WIDE = 512
GAIN_ROWS = 16
EPS = 1e-06
NEG_FILL = -1e30
FACTOR = HD ** (-0.5)
BF = jnp.bfloat16
F32 = jnp.float32

S_AXIS, X_AXIS, Z_AXIS = "section", "dp", "tensor"


def across_x(a, bits):
    n = lax.axis_size(X_AXIS)
    return lax.ppermute(a, X_AXIS, [(i, i ^ bits) for i in range(n)])


def across_z(a):
    return lax.ppermute(a, Z_AXIS, [(0, 1), (1, 0)])


def to_section(a, where):
    n = lax.axis_size(S_AXIS)
    return lax.ppermute(a, S_AXIS, [(i, where(i) % n) for i in range(n)])


def to_section_and(a, where, axis, bits):
    ns, nx = lax.axis_size(S_AXIS), lax.axis_size(axis)
    route = []
    for s in range(ns):
        for x in range(nx):
            route.append((s * nx + x, (where(s) % ns) * nx + (x ^ bits)))
    return lax.ppermute(a, (S_AXIS, axis), route)


def gather_main(own):
    other = across_z(own)
    own1 = across_x(own, 1)
    own3 = across_x(own, 3)
    low = across_x(own3[:2], 1)
    high = across_x(own1[2:], 3)
    other1 = across_x(other, 1)
    other3 = across_x(other, 3)
    other_low = across_z(low)
    other_high = across_z(high)
    return [own, own1, low, high, own3, other, other1, other_low, other_high, other3]


def gather_joined(own, other):
    both = jnp.stack([own, other])
    got1 = across_x(both, 1)
    got3 = across_x(both, 3)
    own2 = across_x(got1[0], 3)
    other2 = across_x(got3[1], 1)
    return [both, got1, got3, own2, other2]


def only(got, unit):
    swap = {2: 3, 7: 8} if unit >= 2 else {3: 2, 8: 7}
    return [got[swap.get(n, n)] for n in range(len(got))]


def piece(refs, k, j, unit):
    if len(refs) == 10:
        if k == 2:
            return (refs[5 * j + 2 + unit // 2], (unit % 2,))
        return (refs[5 * j + {0: 0, 1: 1, 3: 4}[k]], (unit,))
    if k == 2:
        return (refs[3 + j], (unit,))
    return (refs[{0: 0, 1: 1, 3: 2}[k]], (j, unit))


def dot(a, b, ca, cb):
    return lax.dot_general(a, b, (((ca,), (cb,)), ((), ())), preferred_element_type=F32)


def visible_lanes(lens_ref, c):
    x = lax.axis_index(X_AXIS)
    t = lax.axis_index(Z_AXIS)
    length = lens_ref[x ^ c]
    col = lax.broadcasted_iota(jnp.int32, (1, L), 1)
    half = (col >= ROWS).astype(jnp.int32)
    position = col - half * ROWS + ROWS * (half + t - 2 * half * t)
    return position < length


def by_head(a):
    lane = lax.broadcasted_iota(jnp.int32, (1, W), 1)
    zero = jnp.zeros_like(a)
    return jnp.concatenate(
        [jnp.where((lane >= h * HD) & (lane < (h + 1) * HD), a, zero) for h in range(HEADS)], axis=0
    )


def heads_back(a):
    lane = lax.broadcasted_iota(jnp.int32, (1, W), 1)
    out = a[:L]
    for h in range(1, HEADS):
        out = jnp.where(lane >= h * HD, a[h * L : (h + 1) * L], out)
    return out


def normed_rows(refs, unit, gain, normed_ref):
    for i in range(CAPS):
        for j in range(2):
            ref, lead = piece(refs, i, j, unit)
            rows = ref[(*lead, slice(None), slice(None))].astype(F32)
            inverse = lax.rsqrt(jnp.mean(rows * rows, axis=1, keepdims=True) + EPS)
            at = i * L + j * ROWS
            normed_ref[at : at + ROWS, :] = (rows * inverse * gain).astype(BF)


def softmaxed(q, k, seen):
    scores = dot(by_head(q), k, 1, 1) * FACTOR
    scores = jnp.where(seen, scores, NEG_FILL)
    raised = jnp.exp(scores - jnp.max(scores, axis=1, keepdims=True))
    return raised / jnp.sum(raised, axis=1, keepdims=True)


ORDERS = {3: (0, 1, 3, 2), 1: (0, 3, 1, 2)}


def store_split(block, first, tile, keep_ref, send_ref):
    for n, k in enumerate(ORDERS[first]):
        keep_ref[n, :, tile] = block[k * L : k * L + ROWS].astype(BF)
        send_ref[n, :, tile] = block[k * L + ROWS : (k + 1) * L].astype(BF)


def store_flat(block, first, tile, keep_ref, send_ref):
    for n, k in enumerate(ORDERS[first]):
        keep_ref[n, :, tile] = block[k * L : k * L + ROWS].astype(BF)
        send_ref[n * ROWS : (n + 1) * ROWS, tile] = block[k * L + ROWS : (k + 1) * L].astype(BF)


def store_pairs(block, first, tile, keep_ref, send_ref):
    for n, k in enumerate(ORDERS[first]):
        for j in range(2):
            at = k * L + j * ROWS
            ref = send_ref if n >= 2 else keep_ref
            ref[n % 2, j, :, tile] = block[at : at + ROWS].astype(BF)


def forward_kernel(n_pieces, slot, unit, store, first, lens_ref, *refs):
    pieces = refs[:n_pieces]
    gains, wq, wk, wv, wo, keep_ref, send_ref, normed, q_s, k_s, v_s, mix_s = refs[n_pieces:]
    normed_rows(pieces, unit, gains[0, slot : slot + 1, :], normed)
    q_s[...] = dot(normed[...], wq[...], 1, 0).astype(BF)
    k_s[...] = dot(normed[...], wk[...], 1, 0).astype(BF)
    v_s[...] = dot(normed[...], wv[...], 1, 0).astype(BF)
    for c in range(CAPS):
        rows = slice(c * L, (c + 1) * L)
        chances = softmaxed(q_s[rows, :], k_s[rows, :], visible_lanes(lens_ref, c))
        mix_s[rows, :] = heads_back(dot(chances.astype(BF), v_s[rows, :], 1, 0)).astype(BF)
    for n in range(D // WIDE):
        tile = slice(n * WIDE, (n + 1) * WIDE)
        store(dot(mix_s[...], wo[:, tile], 1, 0), first, tile, keep_ref, send_ref)


def backward_kernel(n_pieces, slot, units, first, split, lens_ref, *refs):
    pieces = refs[:n_pieces]
    gains, wq, wk, wv, wo, gain_in = refs[n_pieces : n_pieces + 6]
    refs = refs[n_pieces + 6 :]
    outs, refs = refs[: 4 if split else 2], refs[4 if split else 2 :]
    gain_out, normed, up, dqkv, mix_s, q_s, k_s, v_s, dm_s = refs
    gain = gains[0, slot : slot + 1, :]
    if split:
        outs[1][CAPS * ROWS :, :] = jnp.zeros((GAIN_ROWS, D // 2), BF)
    normed_rows(pieces, units[0], gain, normed)
    for k in range(CAPS):
        for j in range(2):
            ref, lead = piece(pieces, k, j, units[1])
            at = k * L + j * ROWS
            up[at : at + ROWS, :] = ref[(*lead, slice(None), slice(None))]
    q_s[...] = dot(normed[...], wq[...], 1, 0).astype(BF)
    k_s[...] = dot(normed[...], wk[...], 1, 0).astype(BF)
    v_s[...] = dot(normed[...], wv[...], 1, 0).astype(BF)
    dm_s[...] = dot(up[...], wo[...], 1, 1).astype(BF)
    for c in range(CAPS):
        rows = slice(c * L, (c + 1) * L)
        q, k, v = q_s[rows, :], k_s[rows, :], v_s[rows, :]
        chances = softmaxed(q, k, visible_lanes(lens_ref, c))
        weights = chances.astype(BF)
        mix_s[rows, :] = heads_back(dot(weights, v, 1, 0)).astype(BF)
        dm = by_head(dm_s[rows, :])
        grad_chances = dot(dm, v, 1, 1)
        dqkv[rows, 2 * W :] = dot(weights, dm, 0, 0).astype(BF)
        total = jnp.sum(grad_chances * chances, axis=1, keepdims=True)
        grad_scores = (chances * (grad_chances - total) * FACTOR).astype(BF)
        dqkv[rows, :W] = heads_back(dot(grad_scores, k, 1, 0)).astype(BF)
        dqkv[rows, W : 2 * W] = dot(grad_scores, by_head(q), 0, 0).astype(BF)
    for n in range(D // WIDE):
        tile = slice(n * WIDE, (n + 1) * WIDE)
        block = dot(dqkv[:, :W], wq[tile, :], 1, 1)
        block = block + dot(dqkv[:, W : 2 * W], wk[tile, :], 1, 1)
        block = block + dot(dqkv[:, 2 * W :], wv[tile, :], 1, 1)
        part = jnp.sum(block * normed[:, tile].astype(F32), axis=0, keepdims=True)
        row, col = divmod(n * WIDE, D // 2)
        place = (slice(row, row + 1), slice(col, col + WIDE))
        part = gain_in[place] + part / gain[:, tile]
        gain_out[place] = part
        if split:
            outs[1][CAPS * ROWS + row : CAPS * ROWS + row + 1, col : col + WIDE] = part.astype(BF)
        if not split:
            store_split(block, first, tile, *outs)
        elif n < D // WIDE // 2:
            store_flat(block, first, tile, *outs[:2])
        else:
            low = n * WIDE - D // 2
            store_pairs(block, first, slice(low, low + WIDE), *outs[2:])


IN_VMEM = pl.BlockSpec(memory_space=pltpu.VMEM)
IN_SMEM = pl.BlockSpec(memory_space=pltpu.SMEM)


def shape_of(*shape):
    return jax.ShapeDtypeStruct(shape, BF)


def call(kernel, args, outs, scratch, flops):
    return pl.pallas_call(
        kernel,
        in_specs=[IN_SMEM] + [IN_VMEM] * (len(args) - 1),
        out_specs=[IN_VMEM] * len(outs),
        out_shape=outs,
        scratch_shapes=[pltpu.VMEM(s, BF) for s in scratch],
        compiler_params=pltpu.CompilerParams(vmem_limit_bytes=10 * 1024 * 1024),
        cost_estimate=pl.CostEstimate(
            flops=flops, bytes_accessed=8 * 1024 * 1024, transcendentals=TOK * L * 4
        ),
    )(*args)


def forward_call(pieces, unit, lens, weights, slot, first, paired):
    store = store_pairs if paired else store_split
    out = shape_of(2, 2, ROWS, D) if paired else shape_of(CAPS, ROWS, D)

    def kernel(*refs):
        forward_kernel(len(pieces), slot, unit, store, first, *refs)

    return call(
        kernel,
        (lens, *pieces, *weights),
        [out] * 2,
        [(TOK, D)] + [(TOK, W)] * 4,
        2 * TOK * D * W * 4,
    )


def backward_call(pieces, units, lens, weights, slot, gain_in, first, split):
    def kernel(*refs):
        backward_kernel(len(pieces), slot, units, first, split, *refs)

    if split:
        outs = [shape_of(CAPS, ROWS, D // 2), shape_of(CAPS * ROWS + GAIN_ROWS, D // 2)]
        outs += [shape_of(2, 2, ROWS, D // 2)] * 2
    else:
        outs = [shape_of(CAPS, ROWS, D)] * 2
    outs += [jax.ShapeDtypeStruct((2, D // 2), F32)]
    outs += [shape_of(TOK, D)] * 2 + [shape_of(TOK, 3 * W), shape_of(TOK, W)]
    return call(
        kernel, (lens, *pieces, *weights, gain_in), outs, [(TOK, W)] * 4, 2 * TOK * D * W * 8
    )


def weight_grad_kernel(n_ref, u_ref, d_ref, m_ref, *refs):
    outs = refs[-4:]
    block = dot(n_ref[...], d_ref[...], 0, 0)
    blocks = [block[:, n * W : (n + 1) * W] for n in range(3)]
    blocks.append(dot(m_ref[...], u_ref[...], 0, 0))
    for n, out_ref in enumerate(outs):
        total = blocks[n]
        if len(refs) > 4:
            total = total + refs[n][...].astype(F32)
        out_ref[...] = total.astype(BF)


def weight_grad_call(factors, before):
    tile = pl.BlockSpec((TOK, WIDE), lambda n: (0, n))
    whole = lambda width: pl.BlockSpec(
        (TOK, width), lambda n: (0, 0), pipeline_mode=pl.Buffered(1)
    )
    grads = [pl.BlockSpec((None, WIDE, W), lambda n: (0, n, 0))] * 3
    grads += [pl.BlockSpec((None, W, WIDE), lambda n: (0, 0, n))]
    return pl.pallas_call(
        weight_grad_kernel,
        grid=(D // WIDE,),
        in_specs=[tile, tile, whole(3 * W), whole(W)] + (grads if before else []),
        out_specs=grads,
        out_shape=[shape_of(1, D, W)] * 3 + [shape_of(1, W, D)],
        compiler_params=pltpu.CompilerParams(vmem_limit_bytes=14 * 1024 * 1024),
        cost_estimate=pl.CostEstimate(
            flops=2 * TOK * D * W * 4, bytes_accessed=9 * 1024 * 1024, transcendentals=0
        ),
    )(*factors, *before)


def small(kernel, args, outs):
    return pl.pallas_call(
        kernel,
        in_specs=[IN_VMEM] * len(args),
        out_specs=[IN_VMEM] * len(outs),
        out_shape=[jax.ShapeDtypeStruct(*o) for o in outs],
        compiler_params=pltpu.CompilerParams(vmem_limit_bytes=4 * 1024 * 1024),
        cost_estimate=pl.CostEstimate(flops=1 << 20, bytes_accessed=1 << 20, transcendentals=0),
    )(*args)


def halved(keep, came):
    shape = (keep.shape[0] // 2, *keep.shape[1:])
    half = shape[0]
    if half == 1:
        shape = shape[1:]

    def kernel(keep_ref, came_ref, stay_ref, go_ref):
        for n in range(half):
            at = n if half > 1 else slice(None)
            stay_ref[at] = keep_ref[n].astype(F32) + came_ref[n].astype(F32)
            go_ref[at] = (keep_ref[half + n].astype(F32) + came_ref[half + n].astype(F32)).astype(BF)

    return small(kernel, (keep, came), [(shape, F32), (shape, BF)])


def halved_with(keep, came, own, unit):
    shape = keep.shape[1:]

    def kernel(keep_ref, came_ref, own_ref, stay_ref, go_ref):
        stay = keep_ref[0].astype(F32) + came_ref[0].astype(F32)
        stay_ref[...] = (stay + own_ref[unit].astype(F32)).astype(BF)
        go_ref[...] = (keep_ref[1].astype(F32) + came_ref[1].astype(F32)).astype(BF)

    return small(kernel, (keep, came, own), [(shape, BF), (shape, BF)])


def a_stream(keep, send, own, unit, by, first):
    where = lambda s: s + by
    stay, go = halved(keep, across_z(send))
    stay, go = halved_with(stay, across_x(go, first), own, unit)
    one = to_section_and(go, where, X_AXIS, first ^ 2)
    two = to_section(stay, where)
    return (one, two)


def g_stream(keep, send, own, unit, by, first, more):
    where = lambda s: s + by
    stay, go = halved(keep, across_x(send, first))
    came = across_x(go, first ^ 2)
    fill, args = more

    def kernel(keep_ref, came_ref, own_ref, *refs):
        go_ref, two_ref = refs[-2:]
        stay = keep_ref[0].astype(F32) + came_ref[0].astype(F32)
        two_ref[0] = (stay + own_ref[unit].astype(F32)).astype(BF)
        go_ref[...] = (keep_ref[1].astype(F32) + came_ref[1].astype(F32)).astype(BF)
        fill(*refs[:-2], two_ref.at[1])

    go, two = small(kernel, (stay, came, own, *args), [((ROWS, D), BF), ((2, ROWS, D), BF)])
    one = to_section_and(go, where, Z_AXIS, 1)
    return (one, to_section(two, where))


def z_first_parts(keep, send, first):
    stay, go = halved(keep, across_z(send))
    stay, go = halved(stay, across_x(go, first))
    return (stay, across_x(go, first ^ 2))


def halved_with_gain(keep, came, gain):
    half = keep.shape[0] // 2
    shape = (half, ROWS, D // 2)

    def kernel(keep_ref, came_ref, gain_ref, stay_ref, go_ref, total_ref):
        for n in range(half):
            stay_ref[n] = keep_ref[n].astype(F32) + came_ref[n * ROWS : (n + 1) * ROWS].astype(F32)
            other = came_ref[(half + n) * ROWS : (half + n + 1) * ROWS].astype(F32)
            go_ref[n * ROWS : (n + 1) * ROWS] = (keep_ref[half + n].astype(F32) + other).astype(BF)
        at = 2 * half * ROWS
        total = gain_ref[...] + came_ref[at : at + GAIN_ROWS].astype(F32)[:2]
        total_ref[...] = total
        go_ref[half * ROWS :] = jnp.zeros((GAIN_ROWS, D // 2), BF)
        go_ref[half * ROWS : half * ROWS + 2] = total.astype(BF)

    outs = [(shape, F32), ((half * ROWS + GAIN_ROWS, D // 2), BF), (gain.shape, F32)]
    return small(kernel, (keep, came, gain), outs)


def z_first_parts_with_gain(keep, send, gain, first):
    stay, go, gain = halved_with_gain(keep, across_z(send), gain)
    came = across_x(go, first)
    stay, go, gain = halved_with_gain(stay, came, gain)
    return (stay, across_x(go, first ^ 2), gain)


def x_first_parts(keep, send, first):
    stay, go = halved(keep, across_x(send, first))
    stay, go = halved(stay, across_x(go, first ^ 2))
    return (stay, across_z(go))


def input_grad(rows, units, gains, parts):
    width = D // len(parts)

    def fill(both_ref, gain_ref, *refs):
        out_ref = refs[-1]
        rows_ref, up_ref = both_ref.at[units[0]], both_ref.at[units[1]]
        squares = jnp.zeros((ROWS, 1), F32)
        mixed = jnp.zeros((ROWS, 1), F32)
        blocks = []
        for n in range(len(parts)):
            cols = slice(n * width, (n + 1) * width)
            wide = rows_ref[:, cols].astype(F32)
            scaled = refs[2 * n][...].reshape(ROWS, width) + refs[2 * n + 1][:ROWS].astype(F32)
            scaled = scaled * gain_ref[0, :1, cols]
            squares = squares + jnp.sum(wide * wide, axis=1, keepdims=True)
            mixed = mixed + jnp.sum(scaled * wide, axis=1, keepdims=True)
            blocks.append((cols, wide, scaled))
        inverse = lax.rsqrt(squares / D + EPS)
        pull = inverse * inverse * inverse * (mixed / D)
        for cols, wide, scaled in blocks:
            total = up_ref[:, cols].astype(F32) + inverse * scaled - wide * pull
            out_ref[:, cols] = total.astype(BF)

    return (fill, (rows, gains, *[t for pair in parts for t in pair]))


def copied(copies, sem):
    started = []
    for n, (src, dst) in enumerate(copies):
        copy = pltpu.make_async_copy(src, dst, sem.at[n])
        copy.start()
        started.append(copy)
    return started


def pack_main(inputs, cotangents):
    def kernel(in_ref, cot_ref, main_ref, sem):
        copies = [(in_ref.at[0, n], main_ref.at[n]) for n in range(3)]
        for copy in copied([*copies, (cot_ref.at[0, 0], main_ref.at[3])], sem):
            copy.wait()

    return pl.pallas_call(
        kernel,
        name="pack",
        in_specs=[pl.BlockSpec(memory_space=pltpu.HBM)] * 2,
        out_specs=IN_VMEM,
        out_shape=shape_of(4, ROWS, D),
        scratch_shapes=[pltpu.SemaphoreType.DMA((4,))],
        compiler_params=pltpu.CompilerParams(vmem_limit_bytes=65800000),
    )(inputs, cotangents)


def pack_far(inputs, cotangents, lengths):
    def kernel(lens_ref, in_ref, cot_ref, far_ref, sem):
        copies = [(in_ref.at[0, 3], far_ref.at[pl.ds(0, ROWS)])]
        copies += [(cot_ref.at[0, 1], far_ref.at[pl.ds(ROWS, ROWS)])]
        started = copied(copies, sem)
        lane = lax.broadcasted_iota(jnp.int32, (8, D), 1)
        row = jnp.zeros((8, D), jnp.int32)
        for c in range(CAPS):
            row = jnp.where(lane == c, lens_ref[0, 3, c], row)
        far_ref[2 * ROWS :, :] = row.astype(F32).astype(BF)
        for copy in started:
            copy.wait()

    return pl.pallas_call(
        kernel,
        name="pack2",
        in_specs=[IN_SMEM] + [pl.BlockSpec(memory_space=pltpu.HBM)] * 2,
        out_specs=IN_VMEM,
        out_shape=shape_of(2 * ROWS + 8, D),
        scratch_shapes=[pltpu.SemaphoreType.DMA((2,))],
        compiler_params=pltpu.CompilerParams(vmem_limit_bytes=2 * 1024 * 1024),
    )(lengths, inputs, cotangents)


def load(query_weight, key_weight, value_weight, out_weight):
    def kernel(*refs):
        srcs, dsts, sem = refs[:4], refs[4:12], refs[12]
        for copy in copied([(srcs[n % 4].at[0, n // 4], dsts[n]) for n in range(8)], sem):
            copy.wait()

    got = pl.pallas_call(
        kernel,
        name="load",
        in_specs=[pl.BlockSpec(memory_space=pltpu.HBM)] * 4,
        out_specs=[IN_VMEM] * 8,
        out_shape=([shape_of(D, W)] * 3 + [shape_of(W, D)]) * 2,
        scratch_shapes=[pltpu.SemaphoreType.DMA((8,))],
        compiler_params=pltpu.CompilerParams(vmem_limit_bytes=1 << 20),
    )(query_weight, key_weight, value_weight, out_weight)
    return (tuple(got[:4]), tuple(got[4:]))


def gather_out(a_pair, g_pair, e_rows, gain, gain_came):
    def kernel(a1, a2, g1, g2, e1, gain_ref, came_ref, out_ref, gain_out):
        out_ref[0, 0] = (a1[...].astype(F32) + a2[...].astype(F32)).astype(BF)
        out_ref[0, 1] = (g1[...].astype(F32) + g2[0].astype(F32)).astype(BF)
        out_ref[0, 2] = g2[1]
        out_ref[0, 3] = e1[...]
        total = (gain_ref[...] + came_ref[ROWS : ROWS + GAIN_ROWS].astype(F32)[:2]).astype(BF)
        gain_out[:, : D // 2] = total[:1]
        gain_out[:, D // 2 :] = total[1:]

    return pl.pallas_call(
        kernel,
        name="gather_out",
        grid=(1,),
        in_specs=[IN_VMEM] * 7,
        out_specs=[
            pl.BlockSpec((1, 4, ROWS, D), lambda n: (0, 0, 0, 0)),
            pl.BlockSpec((1, D), lambda n: (0, 0)),
        ],
        out_shape=[shape_of(1, 4, ROWS, D), shape_of(1, D)],
        compiler_params=pltpu.CompilerParams(vmem_limit_bytes=8 * 1024 * 1024),
    )(*a_pair, *g_pair, e_rows, gain, gain_came)


def step(
    inputs, cotangents, lengths, query_weight, key_weight, value_weight, out_weight, norm_gain
):
    own_set, other_set = load(query_weight, key_weight, value_weight, out_weight)
    weights, up_weights = (norm_gain, *own_set), (norm_gain, *other_set)
    last = lax.axis_size(S_AXIS) - 1
    mirrored = lambda s: last - s

    main = pack_main(inputs, cotangents)
    far_own = pack_far(inputs, cotangents, lengths)
    main_got = gather_main(main)
    far = to_section(far_own, mirrored)
    far_z = to_section_and(far_own, mirrored, Z_AXIS, 1)[: 2 * ROWS]
    far_lens = far[2 * ROWS, :CAPS].astype(jnp.int32)
    far = far[: 2 * ROWS].reshape(2, ROWS, D)
    far_got = gather_joined(far, far_z.reshape(2, ROWS, D))

    no_gain = jnp.zeros((2, D // 2), F32)
    down_keep, down_send = forward_call(only(main_got, 0), 0, lengths[0, 0], weights, 0, 3, False)
    near_keep, near_send, near_gain, *near_factors = backward_call(
        only(main_got, 2), (2, 3), lengths[0, 2], weights, 0, no_gain, 1, False
    )
    up_keep, up_send = forward_call(only(main_got, 0), 1, lengths[0, 1], up_weights, 1, 3, True)
    keep1, send1, keep2, send2, all_gain, *far_factors = backward_call(
        far_got, (0, 1), far_lens, weights, 0, near_gain, 1, True
    )

    near_parts = z_first_parts(near_keep, near_send, 1)
    near_fill = input_grad(main, (2, 3), norm_gain, [near_parts])
    stay, came, gain = z_first_parts_with_gain(keep1, send1, all_gain, 1)
    far_parts = [(stay, came), x_first_parts(keep2, send2, 1)]
    far_fill, far_args = input_grad(far, (0, 1), norm_gain, far_parts)
    far_grad = small(far_fill, far_args, [((ROWS, D), BF)])[0]
    sent, grad_gain = gather_out(
        a_stream(down_keep, down_send, main, 0, 1, 3),
        g_stream(up_keep, up_send, main, 1, -1, 3, near_fill),
        to_section(far_grad, lambda s: last + 1 - s),
        gain,
        came,
    )
    first_grads = weight_grad_call(near_factors, ())
    grads = weight_grad_call(far_factors, first_grads)
    return (sent, *grads, grad_gain)


def solution(mesh):
    return jax.shard_map(
        step,
        mesh=mesh,
        in_specs=(
            P(S_AXIS, None, (X_AXIS, Z_AXIS), None),
            P(S_AXIS, None, (X_AXIS, Z_AXIS), None),
            P(S_AXIS, None, None),
            P(S_AXIS, None, None, (X_AXIS, Z_AXIS)),
            P(S_AXIS, None, None, (X_AXIS, Z_AXIS)),
            P(S_AXIS, None, None, (X_AXIS, Z_AXIS)),
            P(S_AXIS, None, (X_AXIS, Z_AXIS), None),
            P(S_AXIS, None, None),
        ),
        out_specs=(
            P(S_AXIS, None, (X_AXIS, Z_AXIS), None),
            P(S_AXIS, None, (X_AXIS, Z_AXIS)),
            P(S_AXIS, None, (X_AXIS, Z_AXIS)),
            P(S_AXIS, None, (X_AXIS, Z_AXIS)),
            P(S_AXIS, (X_AXIS, Z_AXIS), None),
            P(S_AXIS, None),
        ),
        check_vma=False,
    )
```
